32 devices in a mesh: gen: 4 (over y, core), rows: 4 (over z), img: 2 (over x).
Axes of the slice: x: 2, y: 2, z: 4, core: 2. Of those that a mesh axis runs over, the one named last changes fastest.
Arguments:
- center: bfloat16 [2, 32, 32, 128], P('img', 'rows'), may hold values from -6 to 6
- gens: bfloat16 [2, 256, 32, 32, 128], P('img', 'gen', 'rows'), may hold values from -6 to 6
- weight: bfloat16 [3, 3, 128, 128], replicated, may hold values from -0.1875 to 0.1875
- bias: float32 [128], replicated, may hold values from -3 to 3
- radius: float32 [2, 32, 32, 128], P('img', 'rows'), may hold values from 1 to 4
- state: int32 [2, 32, 32, 128], P('img', 'rows'), may hold values from 0 to 2, as said below
- unstable: int32 [2, 16384], P('img'), may hold values from 0 to 131071, as said below
- d_center: float32 [2, 32, 32, 128], P('img', 'rows'), may hold values from -6 to 6
- d_gens: bfloat16 [2, 256, 32, 32, 128], P('img', 'gen', 'rows'), may hold values from -6 to 6
- d_new: float32 [2, 16384], P('img'), may hold values from -6 to 6
Outputs:
- grad_center: bfloat16 [2, 32, 32, 128], P('img', 'rows')
- grad_gens: bfloat16 [2, 256, 32, 32, 128], P('img', 'gen', 'rows')
- grad_weight: float32 [3, 3, 128, 128], replicated
- grad_bias: float32 [128], replicated
- grad_radius: float32 [2, 16384], P('img', 'rows')
The draws below stay inside these ranges and needn't reach their ends.
Inputs may be any that keep to these rules, and one draw needn't show every extreme that they name: `unstable`: each row lists 16384 different neurons of its image; 0 and the last neuron are always listed. `state`: 2 exactly at the neurons that the image's row of unstable lists, else 0 or 1.
All inputs are finite; a program needn't handle non-finite values.
Results may differ from the reference program's by a relative error of at most 0.0049.
Values may be sent and summed in bfloat16 or wider, within the bound.
A program may use at most 128 MiB of HBM per device.

```python
import math
import jax
import jax.numpy as jnp
from jax import lax

CH = 128
HEIGHT = 32
WIDTH = 32
UNST = 16384
GENS = 256
IMAGES = 2


def unstable_cells(key, image):
    inner_key = jax.random.fold_in(jax.random.fold_in(key, 7331), image)
    cells = HEIGHT * WIDTH * CH
    inner = jax.random.permutation(jax.random.fold_in(inner_key, 1), cells - 2)[:UNST - 2].astype(jnp.int32) + 1
    ends = jnp.array([0, cells - 1], jnp.int32)
    listed = jnp.concatenate([inner, ends])
    order = jax.random.permutation(jax.random.fold_in(inner_key, 2), UNST)
    return listed[order]


def draw_unstable(key, part):
    return jnp.stack([unstable_cells(key, image) for image in range(IMAGES)]).astype(jnp.int32)


def draw_state(key, part):
    planes = []
    for image in range(IMAGES):
        base = jax.random.randint(jax.random.fold_in(jax.random.fold_in(key, 911), image), (HEIGHT * WIDTH * CH,), 0, 2).astype(jnp.int32)
        base = base.at[unstable_cells(key, image)].set(2)
        planes.append(base.reshape(HEIGHT, WIDTH, CH))
    return jnp.stack(planes).astype(jnp.int32)


def steps_of(own_key, extent, split, low, top_value):
    def one(dim, shards_of):
        steps = jax.random.uniform(jax.random.fold_in(jax.random.fold_in(own_key, 6), dim), (shards_of,), jnp.float32, low / len(split), top_value / len(split))
        return jnp.repeat(jnp.exp(steps), extent[dim] // shards_of).reshape((-1,) + (1,) * (len(extent) - dim - 1))

    level = one(*split[0])
    for cut in split[1:]:
        level = level * one(*cut)
    return level


def noise(key, extent, scale, most, cuts=(), kind=jnp.bfloat16):
    entries = scale * jax.random.normal(key, extent, jnp.float32)
    if cuts:
        entries = entries * steps_of(key, extent, cuts, -0.22, 0.18)
    return jnp.clip(entries, -most, most).astype(kind)


def setup_inputs(seed: int = 0) -> dict:
    splits = jax.random.split(jax.random.key(seed), 11)
    center = noise(splits[0], (IMAGES, HEIGHT, WIDTH, CH), 1.0, 6.0, ((0, 2), (1, 4)))
    gens = noise(splits[1], (IMAGES, GENS, HEIGHT, WIDTH, CH), 1.0, 6.0, ((0, 2), (1, 4), (2, 4)))
    weight = noise(splits[2], (3, 3, CH, CH), (9 * CH) ** -0.5, 0.1875)
    bias = noise(splits[3], (CH,), 0.5, 3.0, (), jnp.float32)
    radius = jnp.clip(jnp.exp(math.log(4.0) - 1.3862944 * jax.random.uniform(splits[4], (IMAGES, HEIGHT, WIDTH, CH), jnp.float32) ** steps_of(splits[4], (IMAGES, HEIGHT, WIDTH, CH), ((0, 2), (1, 4)), -0.2, 0.2)), 1.0, 4.0)
    state = draw_state(jax.random.fold_in(splits[10], 71), 0)
    unstable = draw_unstable(jax.random.fold_in(splits[10], 71), 0)
    d_center = noise(splits[7], (IMAGES, HEIGHT, WIDTH, CH), 1.0, 6.0, ((0, 2), (1, 4)), jnp.float32)
    d_gens = noise(splits[8], (IMAGES, GENS, HEIGHT, WIDTH, CH), 1.0, 6.0, ((0, 2), (1, 4), (2, 4)))
    d_new = noise(splits[9], (IMAGES, UNST), 1.0, 6.0, ((0, 2),), jnp.float32)
    return {"center": center, "gens": gens, "weight": weight, "bias": bias, "radius": radius, "state": state, "unstable": unstable, "d_center": d_center, "d_gens": d_gens, "d_new": d_new}


DIMS = ("NHWC", "HWIO", "NHWC")


def conv_same(field, kernel):
    return lax.conv_general_dilated(field, kernel, (1, 1), ((1, 1), (1, 1)), dimension_numbers=DIMS, preferred_element_type=jnp.float32)


def relu_terms(y_center, products, radius, state, d_center, extra):
    unstable_mask = state == 2
    safe_r = jnp.where(unstable_mask, radius, 1.0)
    two_r = 2.0 * safe_r
    slope = jnp.where(unstable_mask, (y_center + safe_r) / two_r, jnp.where(state == 1, 1.0, 0.0))
    d_mu = d_center + extra
    d_lam = d_center * y_center + products
    d_yc = slope * d_center + jnp.where(unstable_mask, (d_lam - d_mu * y_center) / two_r, 0.0)
    d_rad = jnp.where(unstable_mask, -d_lam * y_center / (two_r * safe_r) + d_mu * (0.25 + y_center * y_center / (two_r * two_r)), 0.0)
    return slope, d_yc, d_rad


def reference(center, gens, weight, bias, radius, state, unstable, d_center, d_gens, d_new):
    flipped = jnp.transpose(weight[::-1, ::-1], (0, 1, 3, 2))
    cells = HEIGHT * WIDTH * CH
    grad_w = jnp.zeros((3, 3, CH, CH), jnp.float32)
    grad_b = jnp.zeros((CH,), jnp.float32)
    centers_out = []
    gens_out = []
    lists_out = []
    for image in range(IMAGES):
        stacked = jnp.concatenate([center[image][None], gens[image]], axis=0)
        forward = conv_same(stacked, weight)
        y_center = forward[0] + bias
        products = jnp.sum(d_gens[image].astype(jnp.float32) * forward[1:], axis=0)
        extra = jnp.zeros((cells,), jnp.float32).at[unstable[image]].add(d_new[image]).reshape(HEIGHT, WIDTH, CH)
        slope, d_yc, d_rad = relu_terms(y_center, products, radius[image], state[image], d_center[image], extra)
        d_all = jnp.concatenate([d_yc.astype(jnp.bfloat16)[None], (slope * d_gens[image].astype(jnp.float32)).astype(jnp.bfloat16)], axis=0)
        backward = conv_same(d_all, flipped).astype(jnp.bfloat16)
        centers_out.append(backward[0])
        gens_out.append(backward[1:])
        padded = jnp.pad(stacked, ((0, 0), (1, 1), (1, 1), (0, 0)))
        flat_d = d_all.reshape(-1, CH)
        taps = []
        for row_off in range(3):
            for col_off in range(3):
                window = padded[:, row_off:row_off + HEIGHT, col_off:col_off + WIDTH, :].reshape(-1, CH)
                taps.append(jnp.dot(window.T, flat_d, preferred_element_type=jnp.float32))
        grad_w = grad_w + jnp.stack(taps).reshape(3, 3, CH, CH)
        grad_b = grad_b + jnp.sum(d_yc, axis=(0, 1))
        lists_out.append(d_rad.reshape(-1)[unstable[image]])
    positions = float(IMAGES * HEIGHT * WIDTH)
    return (jnp.stack(centers_out), jnp.stack(gens_out), grad_w / positions, grad_b / positions, jnp.stack(lists_out))
```

```python
import functools
from types import SimpleNamespace

import jax
import jax.numpy as jnp
from jax import lax
from jax.experimental import pallas as pl
from jax.experimental.pallas import tpu as pltpu
from jax.sharding import PartitionSpec as P

F32 = jnp.float32
BF16 = jnp.bfloat16
I32 = jnp.int32
TN = (((0,), (0,)), ((), ()))
NT = (((1,), (1,)), ((), ()))


def dot(a, b, dims=(((1,), (0,)), ((), ()))):
    return lax.dot_general(a, b, dims, preferred_element_type=F32)


def lanes(parts):
    return jnp.concatenate(parts, axis=1)


def column(count, width):
    return lax.broadcasted_iota(I32, (count, 1), 0) % width


def later(v, col):
    return jnp.where(col == 0, 0.0, pltpu.roll(v, 1, 0))


def sooner(v, col, width):
    return jnp.where(col == width - 1, 0.0, pltpu.roll(v, v.shape[0] - 1, 0))


class Plan:
    def __init__(self, n, band, width, c, listed, gen, rows, img):
        self.n, self.band, self.width, self.c, self.listed = n, band, width, c, listed
        self.gen, self.rows, self.img = gen, rows, img
        self.g = 16 if n % 16 == 0 else n
        self.m = self.g * width
        self.steps = n // self.g
        self.pairs = band // 2
        self.places = band * width
        self.own = self.places // gen
        self.edge = min(self.own, width)
        self.owners = width // self.edge
        self.plane = gen // 2 * img
        pad = 8 * gen * img
        self.parts = [3 * c, 3 * c, 3 * c + pad]
        self.block = listed // rows
        self.sub = self.block // gen
        self.sublines = self.sub // 128
        self.quarter = listed // gen


def layout(p):
    count = [0]

    def take(n):
        count[0] += n
        return count[0] - n

    three = range(3)
    both = dict(
        dup=take(p.steps), ddown=take(p.steps), cup=take(1), cdown=take(1), rup=take(1),
        rdown=take(1), sup=take(1), sdown=take(1), yup=take(1), ydown=take(1),
        extra=take(p.gen), prod=take(p.gen), eup=take(p.gen), edown=take(p.gen),
        dyc=take(p.gen), drad=take(p.gen), list=take(p.gen * p.rows),
        one=[take(1) for _ in three], two=[take(p.plane) for _ in three],
        three=[take(p.rows) for _ in three], four=[take(2 * p.plane) for _ in three],
    )
    remote, count[0] = count[0], 0
    alone = dict(
        x=take(p.steps), d=take(p.steps), center=take(1), weight=take(1),
        bias=take(1), radius=take(1), state=take(1), ids=take(1), dc=take(1), dn=take(1),
    )
    return SimpleNamespace(**both), alone, remote, count[0]


def scratch(p):
    n, b, w, c = p.n, p.band, p.width, p.c
    v = pltpu.VMEM
    _, _, remote, alone = layout(p)
    out = dict(
        x=v((n, b, w, c), BF16),
        d=v((n, b, w, c), BF16),
        top=v((n, w, c), BF16),
        bottom=v((n, w, c), BF16),
        xs=v((2, b, n * w, c), BF16),
        dys=v((3, b + 2, n * w, c), BF16),
        acc=v((4 * c, 6 * c), F32),
        wf=v((12 * c, 2 * c), BF16),
        wb=v((12 * c, 2 * c), BF16),
        wt=v((9 * c, c), BF16),
        weight=v((3, 3, c, c), BF16),
        bias=v((1, c), F32),
        center=v((b + 4, w, c), BF16),
        cs=v((3, (b + 4) * w, c), BF16),
        radius=v((b + 2, w, c), F32),
        state=v((b + 2, w, c), I32),
        slope=v((b + 2, w, c), F32),
        y=v((p.places, c), F32),
        ids=v((1, p.listed), I32),
        dn=v((1, p.listed), F32),
        dc=v((b, w, c), F32),
        extra=v((p.places, c), F32),
        prod=v(((b + 2) * w, c), F32),
        rextra=v((p.gen, p.own, c), F32),
        rprod=v((p.gen, p.own, c), F32),
        rup=v((p.gen, p.edge, c), F32),
        rdown=v((p.gen, p.edge, c), F32),
        dyc=v(((b + 2) * w, c), BF16),
        drad=v((p.places, c), F32),
        sent=v((p.rows, p.sublines, 128), F32),
        list=v((p.gen, p.rows, p.sublines, 128), F32),
    )
    halves = [rows // 2 for rows in p.parts]
    pieces = [half // p.plane for half in halves]
    out.update(
        gw=[v((rows, c), F32) for rows in p.parts],
        one=[v((half, c), F32) for half in halves],
        two=[v((p.plane, piece, c), F32) for piece in pieces],
        three=[v((p.rows, piece, c), F32) for piece in pieces],
        four=[v((2 * p.plane, piece, c), BF16) for piece in pieces],
        send=pltpu.SemaphoreType.DMA((remote,)),
        recv=pltpu.SemaphoreType.DMA((remote,)),
        local=pltpu.SemaphoreType.DMA((alone,)),
    )
    return out


def kernel(p, tree, *refs):
    hbm = SimpleNamespace()
    (hbm.center, hbm.x, hbm.weight, hbm.bias, hbm.radius, hbm.state, hbm.ids, hbm.dc, hbm.d,
     hbm.dn) = refs[:10]
    o_center, o_gens, o_weight, o_list = refs[10:14]
    r = SimpleNamespace(**jax.tree.unflatten(tree, refs[14:]))
    at_sem, alone, _, _ = layout(p)
    named = vars(r)
    sem_of = vars(at_sem)
    n, band, width, c, g = p.n, p.band, p.width, p.c, p.g
    m, steps, pairs, places, own, edge = p.m, p.steps, p.pairs, p.places, p.own, p.edge
    gi, ri, ii = lax.axis_index("gen"), lax.axis_index("rows"), lax.axis_index("img")
    core, yi = gi % 2, gi // 2
    plane_me = yi * p.img + ii
    first_row, last_row = ri == 0, ri == p.rows - 1

    def copy(src, dst, s, q, to):
        gen, rows, img = to
        return pltpu.make_async_remote_copy(
            src_ref=src, dst_ref=dst, send_sem=r.send.at[s], recv_sem=r.recv.at[q],
            device_id={"gen": gen, "rows": rows, "img": img},
            device_id_type=pl.DeviceIdType.MESH,
        )

    def here(src, dst, s):
        return pltpu.make_async_copy(src, dst, r.local.at[s])

    def chunk(i):
        return pl.ds(i * g, g)

    def flat(i):
        return pl.ds(pl.multiple_of(i * m, m), m)

    def ungen(k):
        return (gi + k) % p.gen

    small = dict(
        center=(hbm.center, r.center.at[pl.ds(2, band)]),
        weight=(hbm.weight, r.weight),
        bias=(hbm.bias, r.bias),
        radius=(hbm.radius, r.radius.at[pl.ds(1, band)]),
        state=(hbm.state, r.state.at[pl.ds(1, band)]),
        ids=(hbm.ids, r.ids),
        dc=(hbm.dc, r.dc),
        dn=(hbm.dn, r.dn),
    )
    order = ("ids", "dn", "weight", "center", "bias", "radius", "state", "dc")

    def small_copy(name):
        return here(*small[name], alone[name])

    def big_copy(name, i):
        return here(
            vars(hbm)[name].at[chunk(i)], named[name].at[chunk(i)], alone[name] + i
        )

    for name in order[:3]:
        small_copy(name).start()
    for i in range(steps):
        big_copy("x", i).start()
        big_copy("d", i).start()
    for name in order[3:]:
        small_copy(name).start()

    barrier = pltpu.get_barrier_semaphore()
    total = p.gen * p.rows * p.img
    me = (gi * p.rows + ri) * p.img + ii

    def greet(k, carry):
        other = (me + k) % total
        pl.semaphore_signal(
            barrier, inc=1,
            device_id={
                "gen": other // (p.rows * p.img),
                "rows": other // p.img % p.rows,
                "img": other % p.img,
            },
            device_id_type=pl.DeviceIdType.MESH,
        )
        return carry

    lax.fori_loop(1, total, greet, 0)
    pl.semaphore_wait(barrier, total - 1)

    above, below = (gi, ri - 1, ii), (gi, ri + 1, ii)

    def rows_up():
        return [
            copy(hbm.d.at[chunk(i), 0], r.bottom.at[chunk(i)],
                 at_sem.dup + i, at_sem.dup + i, above)
            for i in range(steps)
        ]

    def edges_up():
        return [
            copy(hbm.center.at[pl.ds(0, 2)], r.center.at[pl.ds(band + 2, 2)],
                 at_sem.cup, at_sem.cup, above),
            copy(hbm.radius.at[pl.ds(0, 1)], r.radius.at[pl.ds(band + 1, 1)],
                 at_sem.rup, at_sem.rup, above),
            copy(hbm.state.at[pl.ds(0, 1)], r.state.at[pl.ds(band + 1, 1)],
                 at_sem.sup, at_sem.sup, above),
        ]

    def rows_down():
        return [
            copy(hbm.d.at[chunk(i), band - 1], r.top.at[chunk(i)],
                 at_sem.ddown + i, at_sem.ddown + i, below)
            for i in range(steps)
        ]

    def edges_down():
        return [
            copy(hbm.center.at[pl.ds(band - 2, 2)], r.center.at[pl.ds(0, 2)],
                 at_sem.cdown, at_sem.cdown, below),
            copy(hbm.radius.at[pl.ds(band - 1, 1)], r.radius.at[pl.ds(0, 1)],
                 at_sem.rdown, at_sem.rdown, below),
            copy(hbm.state.at[pl.ds(band - 1, 1)], r.state.at[pl.ds(0, 1)],
                 at_sem.sdown, at_sem.sdown, below),
        ]

    @pl.when(ri > 0)
    def _():
        for x in edges_up() + rows_up():
            x.start()

    @pl.when(ri < p.rows - 1)
    def _():
        for x in edges_down() + rows_down():
            x.start()

    @pl.when(first_row)
    def _():
        r.top[...] = jnp.zeros_like(r.top)
        r.center[0:2] = jnp.zeros((2, width, c), BF16)
        r.radius[0:1] = jnp.ones((1, width, c), F32)
        r.state[0:1] = jnp.zeros((1, width, c), I32)
        r.dyc[0:width] = jnp.zeros((width, c), BF16)

    @pl.when(last_row)
    def _():
        r.bottom[...] = jnp.zeros_like(r.bottom)
        r.center[band + 2 : band + 4] = jnp.zeros((2, width, c), BF16)
        r.radius[band + 1 : band + 2] = jnp.ones((1, width, c), F32)
        r.state[band + 1 : band + 2] = jnp.zeros((1, width, c), I32)
        r.dyc[(band + 1) * width : (band + 2) * width] = jnp.zeros((width, c), BF16)

    small_copy("ids").wait()
    small_copy("dn").wait()
    row0 = ri * places

    def located(ids):
        place = ids // c - row0
        return place, ids % c

    step = min(p.quarter, 1024)
    r.extra[...] = jnp.zeros_like(r.extra)

    def spread(k, carry):
        at = pl.ds(pl.multiple_of(gi * p.quarter + k * step, step), step)
        place, chan = located(r.ids[:, at])
        value = r.dn[:, at]
        high = value.astype(BF16).astype(F32)
        low = value - high
        at_chan = lax.broadcasted_iota(I32, (c, step), 0) == chan
        terms = jnp.concatenate(
            [jnp.where(at_chan, v, 0.0).astype(BF16) for v in (high, low)], axis=0
        )
        at_place = lax.broadcasted_iota(I32, (places, step), 0) == place
        got = dot(jnp.where(at_place, 1.0, 0.0).astype(BF16), terms, NT)
        r.extra[...] += got[:, :c] + got[:, c:]
        return carry

    lax.fori_loop(0, p.quarter // step, spread, 0)

    def gen_part(name, k):
        other = ungen(k)
        base = width if name == "prod" else 0
        at = pl.ds(pl.multiple_of(base + other * own, 8), own)
        return copy(named[name].at[at], named["r" + name].at[gi], sem_of[name] + other,
                    sem_of[name] + gi, (other, ri, ii))

    def gen_from(name, k):
        other = ungen(k)
        return copy(named["r" + name].at[other], named["r" + name].at[other], sem_of[name] + other,
                    sem_of[name] + other, (other, ri, ii))

    for k in range(1, p.gen):
        gen_part("extra", k).start()

    small_copy("weight").wait()
    for a in range(3):
        for b in range(3):
            at = (a * 3 + b) * c
            r.wt[at : at + c] = r.weight[a, b].astype(F32).T.astype(BF16)
    for j in range(2):
        for b in range(3):
            for k in range(2):
                at = ((j * 3 + b) * 2 + k) * c
                for t in range(2):
                    cols = slice(t * c, (t + 1) * c)
                    a = 2 * j + k - t
                    zero = jnp.zeros((c, c), BF16)
                    r.wf[at : at + c, cols] = r.weight[a, b] if 0 <= a < 3 else zero
                    a = t - 2 * j - k + 2
                    row = (a * 3 + b) * c
                    r.wb[at : at + c, cols] = r.wt[row : row + c] if 0 <= a < 3 else zero

    def x_row(i, b, h):
        if b == 1:
            return r.x[chunk(i), h].reshape(m, c)
        return r.xs[b // 2, h, flat(i), :]

    def d_row(i, h):
        if h < 0:
            return r.top[chunk(i)]
        if h >= band:
            return r.bottom[chunk(i)]
        return r.d[chunk(i), h]

    def products_pair(i, q):
        parts = []
        for k in (q - 1, q):
            if 0 <= k < pairs:
                for b in range(3):
                    parts += [x_row(i, b, 2 * k), x_row(i, b, 2 * k + 1)]
        low = 0 if q > 0 else 6 * c
        high = 12 * c if q < pairs else 6 * c
        y = dot(lanes(parts), r.wf[low:high, :])
        for t in range(2):
            h = 2 * q - 1 + t
            term = d_row(i, h).astype(F32) * y[:, t * c : (t + 1) * c].reshape(g, width, c)
            r.prod[(h + 1) * width : (h + 2) * width] += jnp.sum(term, axis=0)

    r.prod[...] = jnp.zeros_like(r.prod)

    def inner_products(i, carry):
        big_copy("x", i).wait()
        big_copy("d", i).wait()
        col = column(m, width)
        for h in range(band):
            v = r.x[chunk(i), h].reshape(m, c).astype(F32)
            r.xs[0, h, flat(i), :] = later(v, col).astype(BF16)
            r.xs[1, h, flat(i), :] = sooner(v, col, width).astype(BF16)
        for q in range(1, pairs):
            products_pair(i, q)
        return carry

    lax.fori_loop(0, steps, inner_products, 0)

    for name in order[3:]:
        small_copy(name).wait()

    @pl.when(ri < p.rows - 1)
    def _():
        for x in edges_up():
            x.wait_recv()

    @pl.when(ri > 0)
    def _():
        for x in edges_down():
            x.wait_recv()

    wide = (band + 2) * width
    tall = (band + 4) * width
    v = r.center[...].reshape(tall, c).astype(F32)
    col = column(tall, width)
    r.cs[0] = later(v, col).astype(BF16)
    r.cs[1] = v.astype(BF16)
    r.cs[2] = sooner(v, col, width).astype(BF16)
    y = r.bias[...]
    for a in range(3):
        for b in range(3):
            y = y + dot(r.cs[b, a * width : a * width + wide, :], r.weight[a, b])
    r.y[...] = y[width : width + places]
    y = y.reshape(band + 2, width, c)
    unst = r.state[...] == 2
    safe = jnp.where(unst, r.radius[...], 1.0)
    r.slope[...] = jnp.where(
        unst, (y + safe) / (2.0 * safe), jnp.where(r.state[...] == 1, 1.0, 0.0)
    )

    def dy_rows(i, hs):
        col = column(m, width)
        for h in hs:
            f = (d_row(i, h).astype(F32) * r.slope[h + 1][None]).reshape(m, c)
            r.dys[0, h + 1, flat(i), :] = sooner(f, col, width).astype(BF16)
            r.dys[1, h + 1, flat(i), :] = f.astype(BF16)
            r.dys[2, h + 1, flat(i), :] = later(f, col).astype(BF16)

    def x_pair(i, k):
        return lanes([x_row(i, 1, 2 * k), x_row(i, 1, 2 * k + 1)])

    def dy_pair(i, b, q):
        return lanes([r.dys[b, 2 * q, flat(i), :], r.dys[b, 2 * q + 1, flat(i), :]])

    r.acc[...] = jnp.zeros_like(r.acc)

    def inner_weights(i, carry):
        dy_rows(i, range(1, band - 1))
        for b in range(3):
            cols = slice(b * 2 * c, (b + 1) * 2 * c)
            lhs = jnp.concatenate(
                [lanes([x_pair(i, q - 1), x_pair(i, q)]) for q in range(1, pairs)], axis=0
            )
            rhs = jnp.concatenate([dy_pair(i, b, q) for q in range(1, pairs)], axis=0)
            r.acc[:, cols] += dot(lhs, rhs, TN)
        return carry

    lax.fori_loop(0, steps, inner_weights, 0)

    def outer_products(i, carry):
        @pl.when(ri < p.rows - 1)
        def _():
            copy(hbm.d.at[chunk(i), 0], r.bottom.at[chunk(i)],
                 at_sem.dup + i, at_sem.dup + i, above).wait_recv()

        @pl.when(ri > 0)
        def _():
            copy(hbm.d.at[chunk(i), 0], r.top.at[chunk(i)],
                 at_sem.ddown + i, at_sem.ddown + i, below).wait_recv()

        products_pair(i, 0)
        products_pair(i, pairs)
        return carry

    lax.fori_loop(0, steps, outer_products, 0)

    for k in range(1, p.gen):
        gen_part("prod", k).start()

    def edge_up(e):
        return copy(r.prod.at[pl.ds(e * edge, edge)], r.rup.at[gi],
                    at_sem.eup + e, at_sem.eup + gi, (p.gen - p.owners + e, ri - 1, ii))

    def edge_down(e):
        return copy(r.prod.at[pl.ds((band + 1) * width + e * edge, edge)], r.rdown.at[gi],
                    at_sem.edown + e, at_sem.edown + gi, (e, ri + 1, ii))

    @pl.when(ri > 0)
    def _():
        for e in range(p.owners):
            edge_up(e).start()

    @pl.when(ri < p.rows - 1)
    def _():
        for e in range(p.owners):
            edge_down(e).start()

    def outer_weights(i, carry):
        dy_rows(i, (-1, 0, band - 1, band))
        for b in range(3):
            cols = slice(b * 2 * c, (b + 1) * 2 * c)
            r.acc[2 * c :, cols] += dot(x_pair(i, 0), dy_pair(i, b, 0), TN)
            r.acc[: 2 * c, cols] += dot(x_pair(i, pairs - 1), dy_pair(i, b, pairs), TN)
        return carry

    lax.fori_loop(0, steps, outer_weights, 0)

    mine = pl.ds(pl.multiple_of(gi * own, own), own)
    mine_wide = pl.ds(pl.multiple_of(width + gi * own, 16), own)

    def gathered(name, k):
        other = ungen(k)
        at = mine_wide if name == "dyc" else mine
        return copy(named[name].at[at], named[name].at[at], sem_of[name] + other,
                    sem_of[name] + gi, (other, ri, ii))

    def gathered_from(name, k):
        other = ungen(k)
        base = width if name == "dyc" else 0
        at = pl.ds(pl.multiple_of(base + other * own, 16), own)
        return copy(named[name].at[at], named[name].at[at], sem_of[name] + other,
                    sem_of[name] + other, (other, ri, ii))

    def one(k):
        half = p.parts[k] // 2
        away = pl.ds(pl.multiple_of((1 - core) * half, 8), half)
        return copy(r.gw[k].at[away], r.one[k], at_sem.one[k],
                    at_sem.one[k], (yi * 2 + 1 - core, ri, ii))

    def plane_dev(q):
        return (q // p.img * 2 + core, ri, q % p.img)

    def two(k, s):
        other = (plane_me + s) % p.plane
        half = p.parts[k] // 2
        piece = half // p.plane
        at = pl.ds(pl.multiple_of(core * half + other * piece, 8), piece)
        return copy(r.gw[k].at[at], r.two[k].at[plane_me],
                    at_sem.two[k] + other, at_sem.two[k] + plane_me, plane_dev(other))

    def two_from(k, s):
        other = (plane_me + s) % p.plane
        ref = r.two[k].at[other]
        return copy(ref, ref, at_sem.two[k] + other, at_sem.two[k] + other,
                    plane_dev(other))

    def three(k, s):
        other = (ri + s) % p.rows
        ref = r.three[k].at[ri]
        return copy(ref, ref, at_sem.three[k] + other, at_sem.three[k] + ri,
                    (gi, other, ii))

    def three_from(k, s):
        other = (ri + s) % p.rows
        ref = r.three[k].at[other]
        return copy(ref, ref, at_sem.three[k] + other, at_sem.three[k] + other,
                    (gi, other, ii))

    slot_me = core * p.plane + plane_me

    def four_to(s):
        other = (slot_me + s) % (2 * p.plane)
        oc, q = other // p.plane, other % p.plane
        return other, (q // p.img * 2 + oc, ri, q % p.img)

    def four(k, s):
        other, to = four_to(s)
        ref = r.four[k].at[slot_me]
        return copy(ref, ref, at_sem.four[k] + other, at_sem.four[k] + slot_me, to)

    def four_from(k, s):
        other, to = four_to(s)
        ref = r.four[k].at[other]
        return copy(ref, ref, at_sem.four[k] + other, at_sem.four[k] + other, to)

    def finish_center_terms():
        for k in range(1, p.gen):
            gen_from("extra", k).wait_recv()
            gen_from("prod", k).wait_recv()
        r.rprod[gi] = r.prod[mine_wide]
        r.rextra[gi] = r.extra[mine]

        @pl.when((ri > 0) & (gi < p.owners))
        def _():
            for k in range(p.gen):
                copy(r.rdown.at[k], r.rdown.at[k], at_sem.edown, at_sem.edown + k,
                     below).wait_recv()
            r.rprod[gi, 0:edge] += jnp.sum(r.rdown[...], axis=0)

        @pl.when((ri < p.rows - 1) & (gi >= p.gen - p.owners))
        def _():
            for k in range(p.gen):
                copy(r.rup.at[k], r.rup.at[k], at_sem.eup, at_sem.eup + k,
                     above).wait_recv()
            r.rprod[gi, own - edge : own] += jnp.sum(r.rup[...], axis=0)

        products = jnp.sum(r.rprod[...], axis=0)
        extra = jnp.sum(r.rextra[...], axis=0)

        y = r.y[mine]
        rows_own = own // width if own >= width else 0

        def field(name, first):
            if rows_own:
                v = named[name][pl.ds(first + gi * rows_own, rows_own)]
                return v.reshape(own, c)
            per = width // own
            at = pl.ds(pl.multiple_of(gi % per * own, 8), own)
            return named[name][first + gi // per, at]

        state, radius = field("state", 1), field("radius", 1)
        slope, dc = field("slope", 1), field("dc", 0)
        unst = state == 2
        safe = jnp.where(unst, radius, 1.0)
        two_r = 2.0 * safe
        d_mu = dc + extra
        d_lam = dc * y + products
        d_yc = slope * dc + jnp.where(unst, (d_lam - d_mu * y) / two_r, 0.0)
        d_rad = jnp.where(
            unst,
            -d_lam * y / (two_r * safe) + d_mu * (0.25 + y * y / (two_r * two_r)),
            0.0,
        )
        d_yc16 = d_yc.astype(BF16)
        r.dyc[mine_wide] = d_yc16
        r.drad[mine] = d_rad
        for k in range(1, p.gen):
            gathered("dyc", k).start()
            gathered("drad", k).start()
        for b in range(3):
            window = lanes(
                [
                    r.cs[b, pl.ds(pl.multiple_of((a + 1) * width + gi * own, 16), own), :]
                    for a in range(3)
                ]
            )
            gc = dot(window, d_yc16, TN)
            lo, hi = 2 * b * c, (2 * b + 1) * c
            acc = r.acc
            for a, (first, second) in enumerate(
                (
                    ((0, lo), (c, hi)),
                    ((c, lo), (2 * c, hi)),
                    ((2 * c, lo), (3 * c, hi)),
                )
            ):
                r.gw[b][a * c : (a + 1) * c] = (
                    acc[first[0] : first[0] + c, first[1] : first[1] + c]
                    + acc[second[0] : second[0] + c, second[1] : second[1] + c]
                    + gc[a * c : (a + 1) * c]
                )
            if b == 2:
                spare = p.parts[2] - 3 * c
                at_top = lax.broadcasted_iota(I32, (spare, c), 0) == 0
                total_b = jnp.sum(d_yc, axis=0, keepdims=True)
                r.gw[2][3 * c :] = jnp.where(at_top, total_b, 0.0)
            one(b).start()

    def add_one():
        for k in range(3):
            one(k).wait()
            half = p.parts[k] // 2
            at = pl.ds(pl.multiple_of(core * half, 8), half)
            r.gw[k][at] += r.one[k][...]
            for s in range(1, p.plane):
                two(k, s).start()

    def add_two():
        for k in range(3):
            piece = p.parts[k] // 2 // p.plane
            at = pl.ds(
                pl.multiple_of(core * (p.parts[k] // 2) + plane_me * piece, 8), piece
            )
            for s in range(1, p.plane):
                two_from(k, s).wait_recv()
            r.two[k][plane_me] = r.gw[k][at]
            r.three[k][ri] = jnp.sum(r.two[k][...], axis=0)
            for s in range(1, p.rows):
                three(k, s).start()

    positions = float(places * p.rows * p.img)

    def add_three():
        for k in range(3):
            for s in range(1, p.rows):
                three_from(k, s).wait_recv()
            total = jnp.sum(r.three[k][...], axis=0) / positions
            r.four[k][slot_me] = total.astype(BF16)
            for s in range(1, 2 * p.plane):
                four(k, s).start()

    def y_up():
        return copy(r.dyc.at[pl.ds(width, width)],
                    r.dyc.at[pl.ds((band + 1) * width, width)],
                    at_sem.yup, at_sem.yup, above)

    def y_down():
        return copy(r.dyc.at[pl.ds(band * width, width)], r.dyc.at[pl.ds(0, width)],
                    at_sem.ydown, at_sem.ydown, below)

    def share_center():
        for k in range(1, p.gen):
            gathered_from("dyc", k).wait_recv()

        @pl.when(ri > 0)
        def _():
            y_up().start()

        @pl.when(ri < p.rows - 1)
        def _():
            y_down().start()

    def list_copy(q, s):
        gen = (gi + s) % p.gen
        return copy(r.sent.at[q], r.list.at[gi, ri], at_sem.list + q * p.gen + gen,
                    at_sem.list + ri * p.gen + gi, (gen, q, ii))

    def pick_list():
        for k in range(1, p.gen):
            gathered_from("drad", k).wait_recv()
        field = r.drad[...]
        high = field.astype(BF16).astype(F32)
        low = field - high
        both = lanes([high.astype(BF16), low.astype(BF16)])

        def pick(q, carry):
            at = pl.ds(pl.multiple_of(q * p.block + gi * p.sub, p.sub), p.sub)
            place, chan = located(r.ids[:, at])
            at_place = lax.broadcasted_iota(I32, (places, p.sub), 0) == place
            hit = jnp.where(at_place, 1.0, 0.0).astype(BF16)
            got = dot(both, hit, TN)
            got = got[:c] + got[c:]
            at_chan = lax.broadcasted_iota(I32, (c, p.sub), 0) == chan
            found = jnp.sum(jnp.where(at_chan, got, 0.0), axis=0, keepdims=True)
            for k in range(p.sublines):
                r.sent[q, k : k + 1, :] = found[:, k * 128 : (k + 1) * 128]
            return carry

        lax.fori_loop(0, p.rows, pick, 0)
        r.list[gi, ri] = r.sent[ri]
        for q in range(p.rows):
            for s in range(1, p.gen):
                list_copy(q, s).start()

            @pl.when(ri != q)
            def _():
                list_copy(q, 0).start()

    def center_backward():
        @pl.when(ri < p.rows - 1)
        def _():
            y_up().wait_recv()

        @pl.when(ri > 0)
        def _():
            y_down().wait_recv()

        v = r.dyc[...].astype(F32)
        col = column(wide, width)
        shifted = [sooner(v, col, width).astype(BF16), v.astype(BF16), later(v, col).astype(BF16)]
        got = jnp.zeros((places, c), F32)
        for a in range(3):
            for b in range(3):
                at = (2 - a) * width
                row = (a * 3 + b) * c
                got = got + dot(shifted[b][at : at + places], r.wt[row : row + c])
        o_center[...] = got.astype(BF16).reshape(band, width, c)

    units = steps * pairs
    slots = (
        (3, finish_center_terms),
        (6, add_one),
        (7, share_center),
        (8, pick_list),
        (11, add_two),
        (13, center_backward),
    )

    def backward(u, carry):
        i, k = u // pairs, u % pairs
        parts = []
        for j in range(2):
            for b in range(3):
                for t in range(2):
                    parts.append(r.dys[b, 2 * (k + j) + t, flat(i), :])
        y = dot(lanes(parts), r.wb[...])
        for t in range(2):
            o_gens[chunk(i), 2 * k + t] = (
                y[:, t * c : (t + 1) * c].astype(BF16).reshape(g, width, c)
            )

        return carry

    done = 0
    for sixteenth, work in slots:
        at = sixteenth * units // 16
        if at > done:
            lax.fori_loop(done, at, backward, 0)
        work()
        done = at
    lax.fori_loop(done, units, backward, 0)
    add_three()

    for q in range(p.rows):
        for s in range(p.gen):
            gen = (gi + s) % p.gen
            ref = r.list.at[gen, q]
            wait = copy(ref, ref, at_sem.list, at_sem.list + q * p.gen + gen, (gen, q, ii))
            if s:
                wait.wait_recv()
            else:
                pl.when(ri != q)(wait.wait_recv)
    for k in range(p.gen):
        o_list[k * p.sublines : (k + 1) * p.sublines, :] = jnp.sum(r.list[k], axis=0)

    @pl.when(ri > 0)
    def _():
        for x in edges_up() + rows_up():
            x.wait_send()
        for e in range(p.owners):
            edge_up(e).wait_send()
        y_up().wait_send()

    @pl.when(ri < p.rows - 1)
    def _():
        for x in edges_down() + rows_down():
            x.wait_send()
        for e in range(p.owners):
            edge_down(e).wait_send()
        y_down().wait_send()

    for k in range(1, p.gen):
        for name in ("extra", "prod"):
            gen_part(name, k).wait_send()
        for name in ("dyc", "drad"):
            gathered(name, k).wait_send()
    for q in range(p.rows):
        for s in range(1, p.gen):
            list_copy(q, s).wait_send()
        pl.when(ri != q)(list_copy(q, 0).wait_send)
    for k in range(3):
        for s in range(1, p.plane):
            two(k, s).wait_send()
        for s in range(1, p.rows):
            three(k, s).wait_send()
    for k in range(3):
        for s in range(1, 2 * p.plane):
            four_from(k, s).wait_recv()
        o_weight[k, : p.parts[k]] = r.four[k][...].reshape(p.parts[k], c)
        for s in range(1, 2 * p.plane):
            four(k, s).wait_send()


def finish_kernel(gens_in, center_in, weight_in, list_in, gens, center, weight, bias, listed, sem):
    steps = sem.shape[0]
    g = gens.shape[0] // steps
    copies = [
        pltpu.make_async_copy(
            gens_in.at[pl.ds(i * g, g)], gens.at[pl.ds(i * g, g)], sem.at[i]
        )
        for i in range(steps)
    ]
    for x in copies:
        x.start()
    center[...] = center_in[...]
    c = center.shape[-1]
    for b in range(3):
        for a in range(3):
            weight[a, b] = weight_in[b, a * c : (a + 1) * c].astype(F32)
    bias[...] = weight_in[2, 3 * c : 3 * c + 1].astype(F32)
    for k in range(list_in.shape[0]):
        listed[:, k * 128 : (k + 1) * 128] = list_in[k : k + 1, :]
    for x in copies:
        x.wait()


def on_device(center, gens, weight, bias, radius, state, unstable, d_center, d_gens, d_new):
    n, band, width, c = gens.shape[1:]
    gen, rows, img = (lax.axis_size(a) for a in ("gen", "rows", "img"))
    p = Plan(n, band, width, c, unstable.shape[1], gen, rows, img)
    mem, tree = jax.tree.flatten(scratch(p))
    any_spec = pl.BlockSpec(memory_space=pl.ANY)
    vmem = pl.BlockSpec(memory_space=pltpu.VMEM)
    out = pl.pallas_call(
        functools.partial(kernel, p, tree),
        in_specs=[any_spec] * 10,
        out_specs=(vmem,) * 4,
        out_shape=(
            pltpu.VMEM((band, width, c), BF16),
            pltpu.VMEM((n, band, width, c), BF16),
            pltpu.VMEM((3, p.parts[2], c), BF16),
            pltpu.VMEM((p.block // 128, 128), F32),
        ),
        scratch_shapes=mem,
        compiler_params=pltpu.CompilerParams(
            collective_id=0, has_side_effects=True, vmem_limit_bytes=52 * 1024 * 1024
        ),
        name="zonotope",
    )(
        center[0], gens[0], weight, bias[None], radius[0], state[0], unstable, d_center[0],
        d_gens[0], d_new,
    )
    grad_center, grad_gens, grad_weight, grad_list = out
    out = pl.pallas_call(
        finish_kernel,
        in_specs=[vmem] * 4,
        out_specs=(any_spec,) + (vmem,) * 4,
        out_shape=(
            jax.ShapeDtypeStruct((n, band, width, c), BF16),
            jax.ShapeDtypeStruct((band, width, c), BF16),
            jax.ShapeDtypeStruct((3, 3, c, c), F32),
            jax.ShapeDtypeStruct((1, c), F32),
            jax.ShapeDtypeStruct((1, p.block), F32),
        ),
        scratch_shapes=[pltpu.SemaphoreType.DMA((4,))],
        compiler_params=pltpu.CompilerParams(vmem_limit_bytes=16 * 1024 * 1024),
        name="finish",
    )(*(pltpu.with_memory_space_constraint(x, pltpu.VMEM)
        for x in (grad_gens, grad_center, grad_weight, grad_list)))
    grad_gens, grad_center, grad_weight, grad_bias, grad_list = out
    return grad_center[None], grad_gens[None], grad_weight, grad_bias[0], grad_list


def solution(mesh):
    return jax.shard_map(
        on_device,
        mesh=mesh,
        in_specs=(
            P("img", "rows", None, None),
            P("img", "gen", "rows", None, None),
            P(),
            P(),
            P("img", "rows", None, None),
            P("img", "rows", None, None),
            P("img", None),
            P("img", "rows", None, None),
            P("img", "gen", "rows", None, None),
            P("img", None),
        ),
        out_specs=(
            P("img", "rows", None, None),
            P("img", "gen", "rows", None, None),
            P(),
            P(),
            P("img", "rows"),
        ),
        check_vma=False,
    )
```

```python
import functools
from types import SimpleNamespace

import jax
import jax.numpy as jnp
from jax import lax
from jax.experimental import pallas as pl
from jax.experimental.pallas import tpu as pltpu
from jax.sharding import PartitionSpec as P

F32 = jnp.float32
BF16 = jnp.bfloat16
I32 = jnp.int32
TN = (((0,), (0,)), ((), ()))
NT = (((1,), (1,)), ((), ()))


def dot(a, b, dims=(((1,), (0,)), ((), ()))):
    return lax.dot_general(a, b, dims, preferred_element_type=F32)


def lanes(parts):
    return jnp.concatenate(parts, axis=1)


def column(count, width):
    return lax.broadcasted_iota(I32, (count, 1), 0) % width


def later(v, col):
    return jnp.where(col == 0, 0.0, pltpu.roll(v, 1, 0))


def sooner(v, col, width):
    return jnp.where(col == width - 1, 0.0, pltpu.roll(v, v.shape[0] - 1, 0))


class Plan:
    def __init__(self, n, band, width, c, listed, gen, rows, img):
        self.n, self.band, self.width, self.c, self.listed = n, band, width, c, listed
        self.gen, self.rows, self.img = gen, rows, img
        self.g = 16 if n % 16 == 0 else n
        self.m = self.g * width
        self.steps = n // self.g
        self.pairs = band // 2
        self.places = band * width
        self.own = self.places // gen
        self.edge = min(self.own, width)
        self.owners = width // self.edge
        self.plane = gen // 2 * img
        pad = 8 * gen * img
        self.parts = [3 * c, 3 * c, 3 * c + pad]
        self.block = listed // rows
        self.sub = self.block // gen
        self.sublines = self.sub // 128
        self.quarter = listed // gen


def layout(p):
    count = [0]

    def take(n):
        count[0] += n
        return count[0] - n

    three = range(3)
    both = dict(
        dup=take(p.steps), ddown=take(p.steps), cup=take(1), cdown=take(1), rup=take(1),
        rdown=take(1), sup=take(1), sdown=take(1), yup=take(1), ydown=take(1),
        extra=take(p.gen), prod=take(p.gen), eup=take(p.gen), edown=take(p.gen),
        dyc=take(p.gen), drad=take(p.gen), list=take(p.gen * p.rows),
        one=[take(1) for _ in three], two=[take(p.plane) for _ in three],
        three=[take(p.rows) for _ in three], four=[take(2 * p.plane) for _ in three],
    )
    remote, count[0] = count[0], 0
    alone = dict(
        x=take(p.steps), d=take(p.steps), center=take(1), weight=take(1),
        bias=take(1), radius=take(1), state=take(1), ids=take(1), dc=take(1), dn=take(1),
    )
    return SimpleNamespace(**both), alone, remote, count[0]


def scratch(p):
    n, b, w, c = p.n, p.band, p.width, p.c
    v = pltpu.VMEM
    _, _, remote, alone = layout(p)
    out = dict(
        x=v((n, b, w, c), BF16),
        d=v((n, b, w, c), BF16),
        top=v((n, w, c), BF16),
        bottom=v((n, w, c), BF16),
        xs=v((2, b, n * w, c), BF16),
        dys=v((3, b + 2, n * w, c), BF16),
        acc=v((4 * c, 6 * c), F32),
        wf=v((12 * c, 2 * c), BF16),
        wb=v((12 * c, 2 * c), BF16),
        wt=v((9 * c, c), BF16),
        weight=v((3, 3, c, c), BF16),
        bias=v((1, c), F32),
        center=v((b + 4, w, c), BF16),
        cs=v((3, (b + 4) * w, c), BF16),
        radius=v((b + 2, w, c), F32),
        state=v((b + 2, w, c), I32),
        slope=v((b + 2, w, c), F32),
        y=v((p.places, c), F32),
        ids=v((1, p.listed), I32),
        dn=v((1, p.listed), F32),
        dc=v((b, w, c), F32),
        extra=v((p.places, c), F32),
        prod=v(((b + 2) * w, c), F32),
        rextra=v((p.gen, p.own, c), F32),
        rprod=v((p.gen, p.own, c), F32),
        rup=v((p.gen, p.edge, c), F32),
        rdown=v((p.gen, p.edge, c), F32),
        dyc=v(((b + 2) * w, c), BF16),
        drad=v((p.places, c), F32),
        sent=v((p.rows, p.sublines, 128), F32),
        list=v((p.gen, p.rows, p.sublines, 128), F32),
    )
    halves = [rows // 2 for rows in p.parts]
    pieces = [half // p.plane for half in halves]
    out.update(
        gw=[v((rows, c), F32) for rows in p.parts],
        one=[v((half, c), F32) for half in halves],
        two=[v((p.plane, piece, c), F32) for piece in pieces],
        three=[v((p.rows, piece, c), BF16) for piece in pieces],
        four=[v((2 * p.plane, piece, c), BF16) for piece in pieces],
        send=pltpu.SemaphoreType.DMA((remote,)),
        recv=pltpu.SemaphoreType.DMA((remote,)),
        local=pltpu.SemaphoreType.DMA((alone,)),
    )
    return out


def kernel(p, tree, *refs):
    hbm = SimpleNamespace()
    (hbm.center, hbm.x, hbm.weight, hbm.bias, hbm.radius, hbm.state, hbm.ids, hbm.dc, hbm.d,
     hbm.dn) = refs[:10]
    o_center, o_gens, o_weight, o_list = refs[10:14]
    r = SimpleNamespace(**jax.tree.unflatten(tree, refs[14:]))
    at_sem, alone, _, _ = layout(p)
    named = vars(r)
    sem_of = vars(at_sem)
    n, band, width, c, g = p.n, p.band, p.width, p.c, p.g
    m, steps, pairs, places, own, edge = p.m, p.steps, p.pairs, p.places, p.own, p.edge
    gi, ri, ii = lax.axis_index("gen"), lax.axis_index("rows"), lax.axis_index("img")
    core, yi = gi % 2, gi // 2
    plane_me = yi * p.img + ii
    first_row, last_row = ri == 0, ri == p.rows - 1

    def copy(src, dst, s, q, to):
        gen, rows, img = to
        return pltpu.make_async_remote_copy(
            src_ref=src, dst_ref=dst, send_sem=r.send.at[s], recv_sem=r.recv.at[q],
            device_id={"gen": gen, "rows": rows, "img": img},
            device_id_type=pl.DeviceIdType.MESH,
        )

    def here(src, dst, s):
        return pltpu.make_async_copy(src, dst, r.local.at[s])

    def chunk(i, times=1):
        return pl.ds(i * (g * times), g * times)

    def flat(i, times=1):
        return pl.ds(pl.multiple_of(i * (m * times), m), m * times)

    def ungen(k):
        return (gi + k) % p.gen

    small = dict(
        center=(hbm.center, r.center.at[pl.ds(2, band)]),
        weight=(hbm.weight, r.weight),
        bias=(hbm.bias, r.bias),
        radius=(hbm.radius, r.radius.at[pl.ds(1, band)]),
        state=(hbm.state, r.state.at[pl.ds(1, band)]),
        ids=(hbm.ids, r.ids),
        dc=(hbm.dc, r.dc),
        dn=(hbm.dn, r.dn),
    )
    order = ("ids", "dn", "weight", "center", "bias", "radius", "state", "dc")

    def small_copy(name):
        return here(*small[name], alone[name])

    def big_copy(name, i):
        return here(
            vars(hbm)[name].at[chunk(i)], named[name].at[chunk(i)], alone[name] + i
        )

    for name in order[:3]:
        small_copy(name).start()
    for i in range(steps):
        big_copy("x", i).start()
        big_copy("d", i).start()
    for name in order[3:]:
        small_copy(name).start()

    barrier = pltpu.get_barrier_semaphore()
    gens_of = [ungen(k) for k in range(p.gen)]
    rows_of = [ri] + [(ri + k) % p.rows for k in range(1, p.rows)]
    imgs_of = [(ii + k) % p.img for k in range(p.img)]
    peers = [(g_, r_, ii) for g_ in gens_of for r_ in rows_of][1:]
    peers += [(g_, ri, i_) for g_ in gens_of for i_ in imgs_of[1:]]
    for gen_, row_, img_ in peers:
        pl.semaphore_signal(
            barrier, inc=1, device_id={"gen": gen_, "rows": row_, "img": img_},
            device_id_type=pl.DeviceIdType.MESH,
        )

    above, below = (gi, ri - 1, ii), (gi, ri + 1, ii)

    def rows_up():
        return [
            copy(hbm.d.at[chunk(i), 0], r.bottom.at[chunk(i)],
                 at_sem.dup + i, at_sem.dup + i, above)
            for i in range(steps)
        ]

    def edges_up():
        return [
            copy(hbm.center.at[pl.ds(0, 2)], r.center.at[pl.ds(band + 2, 2)],
                 at_sem.cup, at_sem.cup, above),
            copy(hbm.radius.at[pl.ds(0, 1)], r.radius.at[pl.ds(band + 1, 1)],
                 at_sem.rup, at_sem.rup, above),
            copy(hbm.state.at[pl.ds(0, 1)], r.state.at[pl.ds(band + 1, 1)],
                 at_sem.sup, at_sem.sup, above),
        ]

    def rows_down():
        return [
            copy(hbm.d.at[chunk(i), band - 1], r.top.at[chunk(i)],
                 at_sem.ddown + i, at_sem.ddown + i, below)
            for i in range(steps)
        ]

    def edges_down():
        return [
            copy(hbm.center.at[pl.ds(band - 2, 2)], r.center.at[pl.ds(0, 2)],
                 at_sem.cdown, at_sem.cdown, below),
            copy(hbm.radius.at[pl.ds(band - 1, 1)], r.radius.at[pl.ds(0, 1)],
                 at_sem.rdown, at_sem.rdown, below),
            copy(hbm.state.at[pl.ds(band - 1, 1)], r.state.at[pl.ds(0, 1)],
                 at_sem.sdown, at_sem.sdown, below),
        ]

    @pl.when(first_row)
    def _():
        r.top[...] = jnp.zeros_like(r.top)
        r.center[0:2] = jnp.zeros((2, width, c), BF16)
        r.radius[0:1] = jnp.ones((1, width, c), F32)
        r.state[0:1] = jnp.zeros((1, width, c), I32)
        r.dyc[0:width] = jnp.zeros((width, c), BF16)

    @pl.when(last_row)
    def _():
        r.bottom[...] = jnp.zeros_like(r.bottom)
        r.center[band + 2 : band + 4] = jnp.zeros((2, width, c), BF16)
        r.radius[band + 1 : band + 2] = jnp.ones((1, width, c), F32)
        r.state[band + 1 : band + 2] = jnp.zeros((1, width, c), I32)
        r.dyc[(band + 1) * width : (band + 2) * width] = jnp.zeros((width, c), BF16)

    small_copy("ids").wait()
    small_copy("dn").wait()
    row0 = ri * places

    def located(ids):
        place = ids // c - row0
        return place, ids % c

    step = min(p.quarter, 1024)
    r.extra[...] = jnp.zeros_like(r.extra)

    def spread(k, carry):
        at = pl.ds(pl.multiple_of(gi * p.quarter + k * step, step), step)
        place, chan = located(r.ids[:, at])
        value = r.dn[:, at]
        high = value.astype(BF16).astype(F32)
        low = value - high
        at_chan = lax.broadcasted_iota(I32, (c, step), 0) == chan
        terms = jnp.concatenate(
            [jnp.where(at_chan, v, 0.0).astype(BF16) for v in (high, low)], axis=0
        )
        at_place = lax.broadcasted_iota(I32, (places, step), 0) == place
        got = dot(jnp.where(at_place, 1.0, 0.0).astype(BF16), terms, NT)
        r.extra[...] += got[:, :c] + got[:, c:]
        return carry

    lax.fori_loop(0, p.quarter // step, spread, 0)

    def gen_part(name, k):
        other = ungen(k)
        base = width if name == "prod" else 0
        at = pl.ds(pl.multiple_of(base + other * own, 8), own)
        return copy(named[name].at[at], named["r" + name].at[gi], sem_of[name] + other,
                    sem_of[name] + gi, (other, ri, ii))

    def gen_from(name, k):
        other = ungen(k)
        return copy(named["r" + name].at[other], named["r" + name].at[other], sem_of[name] + other,
                    sem_of[name] + other, (other, ri, ii))

    small_copy("weight").wait()
    for a in range(3):
        for b in range(3):
            at = (a * 3 + b) * c
            r.wt[at : at + c] = r.weight[a, b].astype(F32).T.astype(BF16)
    for j in range(2):
        for b in range(3):
            for k in range(2):
                at = ((j * 3 + b) * 2 + k) * c
                for t in range(2):
                    cols = slice(t * c, (t + 1) * c)
                    a = 2 * j + k - t
                    zero = jnp.zeros((c, c), BF16)
                    r.wf[at : at + c, cols] = r.weight[a, b] if 0 <= a < 3 else zero
                    a = t - 2 * j - k + 2
                    row = (a * 3 + b) * c
                    r.wb[at : at + c, cols] = r.wt[row : row + c] if 0 <= a < 3 else zero

    pl.semaphore_wait(barrier, len(peers))

    @pl.when(ri > 0)
    def _():
        for x in edges_up() + rows_up():
            x.start()

    @pl.when(ri < p.rows - 1)
    def _():
        for x in edges_down() + rows_down():
            x.start()

    for k in range(1, p.gen):
        gen_part("extra", k).start()

    def x_row(i, b, h, times=1):
        if b == 1:
            return r.x[chunk(i, times), h].reshape(m * times, c)
        return r.xs[b // 2, h, flat(i, times), :]

    def d_row(i, h, times=1):
        if h < 0:
            return r.top[chunk(i, times)]
        if h >= band:
            return r.bottom[chunk(i, times)]
        return r.d[chunk(i, times), h]

    def products_pair(i, q):
        parts = []
        for k in (q - 1, q):
            if 0 <= k < pairs:
                for b in range(3):
                    parts += [x_row(i, b, 2 * k), x_row(i, b, 2 * k + 1)]
        low = 0 if q > 0 else 6 * c
        high = 12 * c if q < pairs else 6 * c
        y = dot(lanes(parts), r.wf[low:high, :])
        for t in range(2):
            h = 2 * q - 1 + t
            term = d_row(i, h).astype(F32) * y[:, t * c : (t + 1) * c].reshape(g, width, c)
            r.prod[(h + 1) * width : (h + 2) * width] += jnp.sum(term, axis=0)

    r.prod[...] = jnp.zeros_like(r.prod)

    def inner_products(i, carry):
        big_copy("x", i).wait()
        big_copy("d", i).wait()
        col = column(m, width)
        for h in range(band):
            v = r.x[chunk(i), h].reshape(m, c).astype(F32)
            r.xs[0, h, flat(i), :] = later(v, col).astype(BF16)
            r.xs[1, h, flat(i), :] = sooner(v, col, width).astype(BF16)
        for q in range(1, pairs):
            products_pair(i, q)
        return carry

    lax.fori_loop(0, steps, inner_products, 0)

    for name in order[3:]:
        small_copy(name).wait()

    @pl.when(ri < p.rows - 1)
    def _():
        for x in edges_up():
            x.wait_recv()

    @pl.when(ri > 0)
    def _():
        for x in edges_down():
            x.wait_recv()

    wide = (band + 2) * width
    tall = (band + 4) * width
    v = r.center[...].reshape(tall, c).astype(F32)
    col = column(tall, width)
    r.cs[0] = later(v, col).astype(BF16)
    r.cs[1] = v.astype(BF16)
    r.cs[2] = sooner(v, col, width).astype(BF16)
    y = r.bias[...]
    for a in range(3):
        for b in range(3):
            y = y + dot(r.cs[b, a * width : a * width + wide, :], r.weight[a, b])
    r.y[...] = y[width : width + places]
    y = y.reshape(band + 2, width, c)
    unst = r.state[...] == 2
    safe = jnp.where(unst, r.radius[...], 1.0)
    r.slope[...] = jnp.where(
        unst, (y + safe) / (2.0 * safe), jnp.where(r.state[...] == 1, 1.0, 0.0)
    )

    pack = 2 if steps % 2 == 0 else 1

    def dy_rows(i, hs):
        col = column(m * pack, width)
        at = flat(i, pack)
        for h in hs:
            f = (d_row(i, h, pack).astype(F32) * r.slope[h + 1][None]).reshape(m * pack, c)
            r.dys[0, h + 1, at, :] = sooner(f, col, width).astype(BF16)
            r.dys[1, h + 1, at, :] = f.astype(BF16)
            r.dys[2, h + 1, at, :] = later(f, col).astype(BF16)

    def x_pair(i, k):
        return lanes([x_row(i, 1, 2 * k, pack), x_row(i, 1, 2 * k + 1, pack)])

    def dy_pair(i, b, q):
        at = flat(i, pack)
        return lanes([r.dys[b, 2 * q, at, :], r.dys[b, 2 * q + 1, at, :]])

    r.acc[...] = jnp.zeros_like(r.acc)

    def inner_weights(i, carry):
        dy_rows(i, range(1, band - 1))
        for b in range(3):
            cols = slice(b * 2 * c, (b + 1) * 2 * c)
            lhs = jnp.concatenate(
                [lanes([x_pair(i, q - 1), x_pair(i, q)]) for q in range(1, pairs)], axis=0
            )
            rhs = jnp.concatenate([dy_pair(i, b, q) for q in range(1, pairs)], axis=0)
            r.acc[:, cols] += dot(lhs, rhs, TN)
        return carry

    lax.fori_loop(0, steps // pack, inner_weights, 0)

    def outer_products(i, carry):
        @pl.when(ri < p.rows - 1)
        def _():
            copy(hbm.d.at[chunk(i), 0], r.bottom.at[chunk(i)],
                 at_sem.dup + i, at_sem.dup + i, above).wait_recv()

        @pl.when(ri > 0)
        def _():
            copy(hbm.d.at[chunk(i), 0], r.top.at[chunk(i)],
                 at_sem.ddown + i, at_sem.ddown + i, below).wait_recv()

        products_pair(i, 0)
        products_pair(i, pairs)
        return carry

    lax.fori_loop(0, steps, outer_products, 0)

    for k in range(1, p.gen):
        gen_part("prod", k).start()

    def edge_up(e):
        return copy(r.prod.at[pl.ds(e * edge, edge)], r.rup.at[gi],
                    at_sem.eup + e, at_sem.eup + gi, (p.gen - p.owners + e, ri - 1, ii))

    def edge_down(e):
        return copy(r.prod.at[pl.ds((band + 1) * width + e * edge, edge)], r.rdown.at[gi],
                    at_sem.edown + e, at_sem.edown + gi, (e, ri + 1, ii))

    @pl.when(ri > 0)
    def _():
        for e in range(p.owners):
            edge_up(e).start()

    @pl.when(ri < p.rows - 1)
    def _():
        for e in range(p.owners):
            edge_down(e).start()

    def outer_weights(i, carry):
        dy_rows(i, (-1, 0, band - 1, band))
        for b in range(3):
            cols = slice(b * 2 * c, (b + 1) * 2 * c)
            r.acc[2 * c :, cols] += dot(x_pair(i, 0), dy_pair(i, b, 0), TN)
            r.acc[: 2 * c, cols] += dot(x_pair(i, pairs - 1), dy_pair(i, b, pairs), TN)
        return carry

    lax.fori_loop(0, steps // pack, outer_weights, 0)

    mine = pl.ds(pl.multiple_of(gi * own, own), own)
    mine_wide = pl.ds(pl.multiple_of(width + gi * own, 16), own)

    def gathered(name, k):
        other = ungen(k)
        at = mine_wide if name == "dyc" else mine
        return copy(named[name].at[at], named[name].at[at], sem_of[name] + other,
                    sem_of[name] + gi, (other, ri, ii))

    def gathered_from(name, k):
        other = ungen(k)
        base = width if name == "dyc" else 0
        at = pl.ds(pl.multiple_of(base + other * own, 16), own)
        return copy(named[name].at[at], named[name].at[at], sem_of[name] + other,
                    sem_of[name] + other, (other, ri, ii))

    def one(k):
        half = p.parts[k] // 2
        away = pl.ds(pl.multiple_of((1 - core) * half, 8), half)
        return copy(r.gw[k].at[away], r.one[k], at_sem.one[k],
                    at_sem.one[k], (yi * 2 + 1 - core, ri, ii))

    def plane_dev(q):
        return (q // p.img * 2 + core, ri, q % p.img)

    def two(k, s):
        other = (plane_me + s) % p.plane
        half = p.parts[k] // 2
        piece = half // p.plane
        at = pl.ds(pl.multiple_of(core * half + other * piece, 8), piece)
        return copy(r.gw[k].at[at], r.two[k].at[plane_me],
                    at_sem.two[k] + other, at_sem.two[k] + plane_me, plane_dev(other))

    def two_from(k, s):
        other = (plane_me + s) % p.plane
        ref = r.two[k].at[other]
        return copy(ref, ref, at_sem.two[k] + other, at_sem.two[k] + other,
                    plane_dev(other))

    def three(k, s):
        other = (ri + s) % p.rows
        ref = r.three[k].at[ri]
        return copy(ref, ref, at_sem.three[k] + other, at_sem.three[k] + ri,
                    (gi, other, ii))

    def three_from(k, s):
        other = (ri + s) % p.rows
        ref = r.three[k].at[other]
        return copy(ref, ref, at_sem.three[k] + other, at_sem.three[k] + other,
                    (gi, other, ii))

    slot_me = core * p.plane + plane_me

    def four_to(s):
        other = (slot_me + s) % (2 * p.plane)
        oc, q = other // p.plane, other % p.plane
        return other, (q // p.img * 2 + oc, ri, q % p.img)

    def four(k, s):
        other, to = four_to(s)
        ref = r.four[k].at[slot_me]
        return copy(ref, ref, at_sem.four[k] + other, at_sem.four[k] + slot_me, to)

    def four_from(k, s):
        other, to = four_to(s)
        ref = r.four[k].at[other]
        return copy(ref, ref, at_sem.four[k] + other, at_sem.four[k] + other, to)

    def finish_center_terms():
        for k in range(1, p.gen):
            gen_from("extra", k).wait_recv()
            gen_from("prod", k).wait_recv()
        r.rprod[gi] = r.prod[mine_wide]
        r.rextra[gi] = r.extra[mine]

        @pl.when((ri > 0) & (gi < p.owners))
        def _():
            for k in range(p.gen):
                copy(r.rdown.at[k], r.rdown.at[k], at_sem.edown, at_sem.edown + k,
                     below).wait_recv()
            r.rprod[gi, 0:edge] += jnp.sum(r.rdown[...], axis=0)

        @pl.when((ri < p.rows - 1) & (gi >= p.gen - p.owners))
        def _():
            for k in range(p.gen):
                copy(r.rup.at[k], r.rup.at[k], at_sem.eup, at_sem.eup + k,
                     above).wait_recv()
            r.rprod[gi, own - edge : own] += jnp.sum(r.rup[...], axis=0)

        products = jnp.sum(r.rprod[...], axis=0)
        extra = jnp.sum(r.rextra[...], axis=0)

        y = r.y[mine]
        rows_own = own // width if own >= width else 0

        def field(name, first):
            if rows_own:
                v = named[name][pl.ds(first + gi * rows_own, rows_own)]
                return v.reshape(own, c)
            per = width // own
            at = pl.ds(pl.multiple_of(gi % per * own, 8), own)
            return named[name][first + gi // per, at]

        state, radius = field("state", 1), field("radius", 1)
        slope, dc = field("slope", 1), field("dc", 0)
        unst = state == 2
        safe = jnp.where(unst, radius, 1.0)
        two_r = 2.0 * safe
        d_mu = dc + extra
        d_lam = dc * y + products
        d_yc = slope * dc + jnp.where(unst, (d_lam - d_mu * y) / two_r, 0.0)
        d_rad = jnp.where(
            unst,
            -d_lam * y / (two_r * safe) + d_mu * (0.25 + y * y / (two_r * two_r)),
            0.0,
        )
        d_yc16 = d_yc.astype(BF16)
        r.dyc[mine_wide] = d_yc16
        r.drad[mine] = d_rad
        for k in range(1, p.gen):
            gathered("dyc", k).start()
            gathered("drad", k).start()
        for b in range(3):
            window = lanes(
                [
                    r.cs[b, pl.ds(pl.multiple_of((a + 1) * width + gi * own, 16), own), :]
                    for a in range(3)
                ]
            )
            gc = dot(window, d_yc16, TN)
            lo, hi = 2 * b * c, (2 * b + 1) * c
            acc = r.acc
            for a, (first, second) in enumerate(
                (
                    ((0, lo), (c, hi)),
                    ((c, lo), (2 * c, hi)),
                    ((2 * c, lo), (3 * c, hi)),
                )
            ):
                r.gw[b][a * c : (a + 1) * c] = (
                    acc[first[0] : first[0] + c, first[1] : first[1] + c]
                    + acc[second[0] : second[0] + c, second[1] : second[1] + c]
                    + gc[a * c : (a + 1) * c]
                )
            if b == 2:
                spare = p.parts[2] - 3 * c
                at_top = lax.broadcasted_iota(I32, (spare, c), 0) == 0
                total_b = jnp.sum(d_yc, axis=0, keepdims=True)
                r.gw[2][3 * c :] = jnp.where(at_top, total_b, 0.0)
            one(b).start()

    def add_one():
        for k in range(3):
            one(k).wait()
            half = p.parts[k] // 2
            at = pl.ds(pl.multiple_of(core * half, 8), half)
            r.gw[k][at] += r.one[k][...]
            for s in range(1, p.plane):
                two(k, s).start()

    def add_two(k):
        piece = p.parts[k] // 2 // p.plane
        at = pl.ds(pl.multiple_of(core * (p.parts[k] // 2) + plane_me * piece, 8), piece)
        for s in range(1, p.plane):
            two_from(k, s).wait_recv()
        r.two[k][plane_me] = r.gw[k][at]
        r.three[k][ri] = jnp.sum(r.two[k][...], axis=0).astype(BF16)
        for s in range(1, p.rows):
            three(k, s).start()

    positions = float(places * p.rows * p.img)

    def add_three(k):
        for s in range(1, p.rows):
            three_from(k, s).wait_recv()
        total = jnp.sum(r.three[k][...].astype(F32), axis=0) / positions
        r.four[k][slot_me] = total.astype(BF16)
        for s in range(1, 2 * p.plane):
            four(k, s).start()

    def y_up():
        return copy(r.dyc.at[pl.ds(width, width)],
                    r.dyc.at[pl.ds((band + 1) * width, width)],
                    at_sem.yup, at_sem.yup, above)

    def y_down():
        return copy(r.dyc.at[pl.ds(band * width, width)], r.dyc.at[pl.ds(0, width)],
                    at_sem.ydown, at_sem.ydown, below)

    def share_center():
        for k in range(1, p.gen):
            gathered_from("dyc", k).wait_recv()

        @pl.when(ri > 0)
        def _():
            y_up().start()

        @pl.when(ri < p.rows - 1)
        def _():
            y_down().start()

    def list_copy(q, s):
        gen = (gi + s) % p.gen
        return copy(r.sent.at[q], r.list.at[gi, ri], at_sem.list + q * p.gen + gen,
                    at_sem.list + ri * p.gen + gi, (gen, q, ii))

    def pick_list():
        for k in range(1, p.gen):
            gathered_from("drad", k).wait_recv()
        field = r.drad[...]
        high = field.astype(BF16).astype(F32)
        low = field - high
        both = lanes([high.astype(BF16), low.astype(BF16)])

        def pick(q, carry):
            at = pl.ds(pl.multiple_of(q * p.block + gi * p.sub, p.sub), p.sub)
            place, chan = located(r.ids[:, at])
            at_place = lax.broadcasted_iota(I32, (places, p.sub), 0) == place
            hit = jnp.where(at_place, 1.0, 0.0).astype(BF16)
            got = dot(both, hit, TN)
            got = got[:c] + got[c:]
            at_chan = lax.broadcasted_iota(I32, (c, p.sub), 0) == chan
            found = jnp.sum(jnp.where(at_chan, got, 0.0), axis=0, keepdims=True)
            for k in range(p.sublines):
                r.sent[q, k : k + 1, :] = found[:, k * 128 : (k + 1) * 128]
            return carry

        lax.fori_loop(0, p.rows, pick, 0)
        r.list[gi, ri] = r.sent[ri]
        for q in range(p.rows):
            for s in range(1, p.gen):
                list_copy(q, s).start()

            @pl.when(ri != q)
            def _():
                list_copy(q, 0).start()

    def center_backward():
        @pl.when(ri < p.rows - 1)
        def _():
            y_up().wait_recv()

        @pl.when(ri > 0)
        def _():
            y_down().wait_recv()

        v = r.dyc[...].astype(F32)
        col = column(wide, width)
        shifted = [sooner(v, col, width).astype(BF16), v.astype(BF16), later(v, col).astype(BF16)]
        got = jnp.zeros((places, c), F32)
        for a in range(3):
            for b in range(3):
                at = (2 - a) * width
                row = (a * 3 + b) * c
                got = got + dot(shifted[b][at : at + places], r.wt[row : row + c])
        o_center[...] = got.astype(BF16).reshape(band, width, c)

    lumps = max(pairs // 2, 1)
    units = steps * lumps
    slots = (
        (0, finish_center_terms),
        (2, add_one),
        (3, share_center),
        (3, pick_list),
        (4, lambda: add_two(0)),
        (5, lambda: add_two(1)),
        (6, lambda: add_two(2)),
        (6, center_backward),
        (7, lambda: add_three(0)),
    )

    def backward(u, carry):
        i, lump = u // lumps, u % lumps
        for one_of in range(pairs // lumps):
            k = lump * (pairs // lumps) + one_of
            parts = []
            for j in range(2):
                for b in range(3):
                    for t in range(2):
                        parts.append(r.dys[b, 2 * (k + j) + t, flat(i), :])
            y = dot(lanes(parts), r.wb[...])
            for t in range(2):
                o_gens[chunk(i), 2 * k + t] = (
                    y[:, t * c : (t + 1) * c].astype(BF16).reshape(g, width, c)
                )
        return carry

    done = 0
    for eighth, work in slots:
        at = eighth * units // 8
        if at > done:
            lax.fori_loop(done, at, backward, 0)
        work()
        done = at
    lax.fori_loop(done, units, backward, 0)
    add_three(1)

    for q in range(p.rows):
        for s in range(p.gen):
            gen = (gi + s) % p.gen
            ref = r.list.at[gen, q]
            wait = copy(ref, ref, at_sem.list, at_sem.list + q * p.gen + gen, (gen, q, ii))
            if s:
                wait.wait_recv()
            else:
                pl.when(ri != q)(wait.wait_recv)
    add_three(2)
    for k in range(p.gen):
        o_list[k * p.sublines : (k + 1) * p.sublines, :] = jnp.sum(r.list[k], axis=0)

    @pl.when(ri > 0)
    def _():
        for x in edges_up() + rows_up():
            x.wait_send()
        for e in range(p.owners):
            edge_up(e).wait_send()
        y_up().wait_send()

    @pl.when(ri < p.rows - 1)
    def _():
        for x in edges_down() + rows_down():
            x.wait_send()
        for e in range(p.owners):
            edge_down(e).wait_send()
        y_down().wait_send()

    for k in range(1, p.gen):
        for name in ("extra", "prod"):
            gen_part(name, k).wait_send()
        for name in ("dyc", "drad"):
            gathered(name, k).wait_send()
    for q in range(p.rows):
        for s in range(1, p.gen):
            list_copy(q, s).wait_send()
        pl.when(ri != q)(list_copy(q, 0).wait_send)
    for k in range(3):
        for s in range(1, p.plane):
            two(k, s).wait_send()
        for s in range(1, p.rows):
            three(k, s).wait_send()
    for k in range(3):
        for s in range(1, 2 * p.plane):
            four_from(k, s).wait_recv()
        o_weight[k, : p.parts[k]] = r.four[k][...].reshape(p.parts[k], c)
        for s in range(1, 2 * p.plane):
            four(k, s).wait_send()


def finish_kernel(gens_in, center_in, weight_in, list_in, gens, center, weight, bias, listed, sem):
    steps = sem.shape[0]
    g = gens.shape[0] // steps
    copies = [
        pltpu.make_async_copy(
            gens_in.at[pl.ds(i * g, g)], gens.at[pl.ds(i * g, g)], sem.at[i]
        )
        for i in range(steps)
    ]
    for x in copies:
        x.start()
    center[...] = center_in[...]
    c = center.shape[-1]
    for b in range(3):
        for a in range(3):
            weight[a, b] = weight_in[b, a * c : (a + 1) * c].astype(F32)
    bias[...] = weight_in[2, 3 * c : 3 * c + 1].astype(F32)
    for k in range(list_in.shape[0]):
        listed[:, k * 128 : (k + 1) * 128] = list_in[k : k + 1, :]
    for x in copies:
        x.wait()


def on_device(center, gens, weight, bias, radius, state, unstable, d_center, d_gens, d_new):
    n, band, width, c = gens.shape[1:]
    gen, rows, img = (lax.axis_size(a) for a in ("gen", "rows", "img"))
    p = Plan(n, band, width, c, unstable.shape[1], gen, rows, img)
    mem, tree = jax.tree.flatten(scratch(p))
    any_spec = pl.BlockSpec(memory_space=pl.ANY)
    vmem = pl.BlockSpec(memory_space=pltpu.VMEM)
    out = pl.pallas_call(
        functools.partial(kernel, p, tree),
        in_specs=[any_spec] * 10,
        out_specs=(vmem,) * 4,
        out_shape=(
            pltpu.VMEM((band, width, c), BF16),
            pltpu.VMEM((n, band, width, c), BF16),
            pltpu.VMEM((3, p.parts[2], c), BF16),
            pltpu.VMEM((p.block // 128, 128), F32),
        ),
        scratch_shapes=mem,
        compiler_params=pltpu.CompilerParams(
            collective_id=0, has_side_effects=True, vmem_limit_bytes=52 * 1024 * 1024
        ),
        name="zonotope",
    )(
        center[0], gens[0], weight, bias[None], radius[0], state[0], unstable, d_center[0],
        d_gens[0], d_new,
    )
    grad_center, grad_gens, grad_weight, grad_list = out
    out = pl.pallas_call(
        finish_kernel,
        in_specs=[vmem] * 4,
        out_specs=(any_spec,) + (vmem,) * 4,
        out_shape=(
            jax.ShapeDtypeStruct((n, band, width, c), BF16),
            jax.ShapeDtypeStruct((band, width, c), BF16),
            jax.ShapeDtypeStruct((3, 3, c, c), F32),
            jax.ShapeDtypeStruct((1, c), F32),
            jax.ShapeDtypeStruct((1, p.block), F32),
        ),
        scratch_shapes=[pltpu.SemaphoreType.DMA((4,))],
        compiler_params=pltpu.CompilerParams(vmem_limit_bytes=16 * 1024 * 1024),
        name="finish",
    )(*(pltpu.with_memory_space_constraint(x, pltpu.VMEM)
        for x in (grad_gens, grad_center, grad_weight, grad_list)))
    grad_gens, grad_center, grad_weight, grad_bias, grad_list = out
    return grad_center[None], grad_gens[None], grad_weight, grad_bias[0], grad_list


def solution(mesh):
    return jax.shard_map(
        on_device,
        mesh=mesh,
        in_specs=(
            P("img", "rows", None, None),
            P("img", "gen", "rows", None, None),
            P(),
            P(),
            P("img", "rows", None, None),
            P("img", "rows", None, None),
            P("img", None),
            P("img", "rows", None, None),
            P("img", "gen", "rows", None, None),
            P("img", None),
        ),
        out_specs=(
            P("img", "rows", None, None),
            P("img", "gen", "rows", None, None),
            P(),
            P(),
            P("img", "rows"),
        ),
        check_vma=False,
    )
```
